32 devices in a mesh: row: 8 (over z, core), col: 4 (over y, x).
Axes of the slice: x: 2, y: 2, z: 4, core: 2. Of those that a mesh axis runs over, the one named last changes fastest.
Arguments:
- grad: bfloat16 [2, 6144, 24576], P(None, 'row', 'col'), may hold values from -45 to 45, as said below
- memory: float32 [2, 6144, 24576], P(None, 'row', 'col'), may hold values from -6 to 6
- p_prev: float32 [2, 6144, 32], P(None, ('row', 'col')), may hold values from -6 to 6
- q_prev: float32 [2, 24576, 32], P(None, ('col', 'row')), may hold values from -1 to 1
Outputs:
- p_new: float32 [2, 6144, 32], P(None, ('row', 'col'))
- q_new: float32 [2, 24576, 32], P(None, ('col', 'row'))
- error: float32 [2, 6144, 24576], P(None, 'row', 'col')
The draws below stay inside these ranges and needn't reach their ends.
Inputs may be any that keep to these rules, and one draw needn't show every extreme that they name: `grad`: real-valued gradient entries.
All inputs are finite; a program needn't handle non-finite values.
Results may differ from the reference program's by a relative error of at most 0.0003.
Values sent between devices are 32-bit elements; how exact they have to be, the bound alone decides.
A program may use at most 192 MiB of HBM per device.

```python
import jax
import jax.numpy as jnp
from jax import lax

D = 6144
FF = 24576
R = 32
LAYERS = 2


def draw_grad(key, part):
    key_base = jax.random.fold_in(key, 11)
    key_rows = jax.random.fold_in(key, 12)
    key_cols = jax.random.fold_in(key, 13)
    base = jnp.clip(jax.random.normal(key_base, (LAYERS, D, FF), jnp.float32), -5.0, 5.0)
    row_scale = jnp.exp(jax.random.uniform(key_rows, (LAYERS, D, 1), jnp.float32, -1.2, 1.1))
    col_scale = jnp.exp(jax.random.uniform(key_cols, (LAYERS, 1, FF), jnp.float32, -1.2, 1.1))
    return (base * row_scale * col_scale).astype(jnp.bfloat16)


def levels(own_key, extent, split, least, largest):
    level, own = 1.0, jax.random.fold_in(own_key, 6)
    for dim, parts in split:
        steps = jnp.exp(jax.random.uniform(jax.random.fold_in(own, dim), (parts,), jnp.float32, least / len(split), largest / len(split)))
        level = level * jnp.repeat(steps, extent[dim] // parts).reshape([-1 if axis == dim else 1 for axis in range(len(extent))])
    return level


def bell_draw(rng, extent, width, most, pieces=(), held_as=jnp.bfloat16):
    entries = width * jax.random.normal(rng, extent, jnp.float32)
    if pieces:
        entries = entries * levels(rng, extent, pieces, -0.22, 0.18)
    return jnp.clip(entries, -most, most).astype(held_as)


def setup_inputs(seed: int = 0) -> dict:
    key_of = jax.random.split(jax.random.key(seed), 5)
    grad = draw_grad(jax.random.fold_in(key_of[4], 71), 0)
    memory = bell_draw(key_of[1], (LAYERS, D, FF), 1.0, 6.0, ((1, 8), (2, 4)), jnp.float32)
    p_prev = bell_draw(key_of[2], (LAYERS, D, R), 1.0, 6.0, ((1, 32),), jnp.float32)
    q_prev = bell_draw(key_of[3], (LAYERS, FF, R), R ** -0.5, 1.0, ((1, 32),), jnp.float32)
    return {"grad": grad, "memory": memory, "p_prev": p_prev, "q_prev": q_prev}


def reference(grad, memory, p_prev, q_prev):
    lefts = []
    rights = []
    errors = []
    for layer in range(LAYERS):
        approx = jnp.dot(p_prev[layer], q_prev[layer].T, precision=lax.Precision.HIGHEST)
        merged = grad[layer].astype(jnp.float32) + memory[layer] - approx
        left = jnp.dot(merged, q_prev[layer], precision=lax.Precision.HIGHEST)
        gram = jnp.dot(left.T, left, precision=lax.Precision.HIGHEST)
        factor = jnp.linalg.cholesky(gram)
        p_hat = lax.linalg.triangular_solve(factor, left, left_side=False, lower=True, transpose_a=True)
        right = jnp.dot(merged.T, p_hat, precision=lax.Precision.HIGHEST)
        error = merged - jnp.dot(p_hat, right.T, precision=lax.Precision.HIGHEST)
        lefts.append(p_hat)
        rights.append(right)
        errors.append(error)
    return (jnp.stack(lefts), jnp.stack(rights), jnp.stack(errors))
```

```python
import functools

import jax
import jax.numpy as jnp
from jax import lax
from jax.experimental import pallas as pl
from jax.experimental.pallas import tpu as pltpu
from jax.sharding import PartitionSpec as P

MESH = pl.DeviceIdType.MESH
HIGHEST = lax.Precision.HIGHEST
NT = (((1,), (1,)), ((), ()))
NN = (((1,), (0,)), ((), ()))
VMEM_BYTES = 67043328


def dot(a, b, dims=NN, precision=None):
    return lax.dot_general(a, b, dims, precision=precision, preferred_element_type=jnp.float32)


def split(x):
    hi = x.astype(jnp.bfloat16)
    return hi, (x - hi.astype(jnp.float32)).astype(jnp.bfloat16)


def row_tile(rows):
    return next(t for t in (256, 128, 64, 32, 16) if rows % t == 0)


def eye(rows, cols, start):
    i = lax.broadcasted_iota(jnp.int32, (rows, cols), 0) + start
    return (i == lax.broadcasted_iota(jnp.int32, (rows, cols), 1)).astype(jnp.float32)


def inverse_factor(gram):
    k = gram.shape[0]
    both = jnp.concatenate([gram, eye(k, k, 0)], axis=1)
    rows = lax.broadcasted_iota(jnp.int32, both.shape, 0)
    scale = jnp.zeros_like(both)
    for i in range(k):
        pivot = both[i : i + 1, :]
        top = both[i : i + 1, i : i + 1]
        scale = jnp.where(rows == i, lax.rsqrt(top), scale)
        both = both - jnp.where(rows > i, both[:, i : i + 1] / top, 0.0) * pivot
    return (both * scale)[:, k:]


def exchange_kernel(nr, nc, layers, grad, memory, pt, qt, merged, pcat_out, pt_out, qnew,
                    mbuf, gbuf, pslot, qslot, pcat, qcat, acc, left, lhl, gram, rpart, rsib, rz, linv,
                    s_in, s_grad, s_out, sp_s, sp_r, sq_s, sq_r, sf_s, sl_s, sl_r, sg_s, sg_r,
                    ss_s, ss_r, sz_s, sz_r, sn_s, sn_r, sm_s):
    row, col = lax.axis_index("row"), lax.axis_index("col")
    nz = nr // 2
    z, core = row // 2, lax.rem(row, 2)
    sib = z * 2 + (1 - core)
    rank = qt.shape[1]
    width = qt.shape[2]
    rows = mbuf.shape[1]
    share = pt.shape[2]
    tile = row_tile(rows)

    def cols(j):
        return pl.ds(pl.multiple_of(j * width, width), width)

    def peer(dz):
        return lax.rem(z + dz, nz)

    def send(src, dst, ss, rs, **where):
        return pltpu.make_async_remote_copy(src_ref=src, dst_ref=dst, send_sem=ss, recv_sem=rs,
                                            device_id=where, device_id_type=MESH)

    def order(k):
        return peer(k // 2) * 2 + lax.rem(core + lax.rem(k, 2), 2)

    def fetch_mem(l, j):
        return pltpu.make_async_copy(memory.at[l, :, cols(j)], mbuf.at[l, :, cols(j)], s_in.at[l, j])

    def fetch_grad(l, j):
        return pltpu.make_async_copy(grad.at[l, :, cols(j)], gbuf.at[:, cols(j)], s_grad.at[l, j])

    def put(l, j):
        return pltpu.make_async_copy(mbuf.at[l, :, cols(j)], merged.at[l, :, cols(j)], s_out.at[l, j])

    def begin(k, _):
        fetch_mem(0, order(k)).start()
        fetch_grad(0, order(k)).start()
        return 0

    lax.fori_loop(0, nr, begin, 0)

    def begin_next(k, _):
        fetch_mem(1, order(k)).start()
        return 0

    lax.fori_loop(0, nr, begin_next, 0)

    for l in range(layers):
        gram[l, row] = jnp.zeros(gram.shape[2:], jnp.float32)
    barrier = pltpu.get_barrier_semaphore()
    for d in range(1, nr):
        pl.semaphore_signal(barrier, inc=1, device_id={"row": lax.rem(row + d, nr)}, device_id_type=MESH)
    for d in range(1, nc):
        pl.semaphore_signal(barrier, inc=1, device_id={"col": lax.rem(col + d, nc)}, device_id_type=MESH)
    pl.semaphore_wait(barrier, nr + nc - 2)

    def p_copy(c):
        return send(pt, pslot.at[col], sp_s.at[c], sp_r.at[col], col=c)

    def q_copy(r, slot):
        return send(qt, qslot.at[slot], sq_s.at[r], sq_r.at[slot], row=r)

    def q_forward(slot):
        return send(qslot.at[slot], qslot.at[slot], sf_s.at[slot], sq_r.at[slot], row=sib)

    q_copy(sib, row).start()
    for d in range(1, nz):
        q_copy(peer(d) * 2 + core, row).start()
    for d in range(1, nc):
        p_copy(lax.rem(col + d, nc)).start()
    qslot[row] = qt[...]
    pslot[col] = pt[...]
    for d in range(1, nc):
        c = lax.rem(col + d, nc)
        send(pt, pslot.at[c], sp_s.at[c], sp_r.at[c], col=c).wait_recv()
    for l in range(layers):
        for c in range(nc):
            hi, lo = split(pslot[c, l])
            turned = dot(eye(share, share, 0).astype(jnp.bfloat16), jnp.concatenate([hi, lo, hi], axis=0), NT)
            pcat[l, c * share : (c + 1) * share, :] = turned.astype(jnp.bfloat16)
    acc[...] = jnp.zeros_like(acc)

    def first(l):
        def step(k, _):
            j = order(k)
            if l == 0:
                @pl.when(k > 0)
                def _():
                    q_copy(j, j).wait_recv()

                @pl.when(jnp.logical_and(k > 0, lax.rem(k, 2) == 0))
                def _():
                    q_forward(j).start()
            hi, lo = split(qslot[j, l])
            qcat[0:rank, :] = hi
            qcat[rank : 2 * rank, :] = lo
            qcat[2 * rank :, :] = hi
            fetch_mem(l, j).wait()
            fetch_grad(l, j).wait()

            def part(t, _):
                at = pl.ds(pl.multiple_of(t * tile, tile), tile)
                both = qcat[...]
                approx = dot(pcat[l, at, :], jnp.concatenate([both[0:rank], both[2 * rank :], both[rank : 2 * rank]], axis=0))
                m = gbuf[at, cols(j)].astype(jnp.float32) + mbuf[l, at, cols(j)] - approx
                mbuf[l, at, cols(j)] = m
                mh, ml = split(m)
                acc[l, at, :] += dot(mh, both[0 : 2 * rank], NT) + dot(ml, both[0 : 2 * rank], NT)
                return 0

            lax.fori_loop(0, rows // tile, part, 0)
            put(l, j).start()
            if l + 1 < layers:
                fetch_grad(l + 1, j).start()
            return 0

        lax.fori_loop(0, nr, step, 0)
        fold = jnp.concatenate([eye(rank, rank, 0), eye(rank, rank, 0)], axis=1)
        left[l, col] = dot(fold, acc[l], NT, HIGHEST)
        for d in range(1, nc):
            c = lax.rem(col + d, nc)
            send(left.at[l, col], left.at[l, col], sl_s.at[l, c], sl_r.at[l, col], col=c).start()

    def join_left(l):
        for d in range(1, nc):
            c = lax.rem(col + d, nc)
            send(left.at[l, c], left.at[l, c], sl_s.at[l, c], sl_r.at[l, c], col=c).wait()
        total = left[l, 0]
        for c in range(1, nc):
            total = total + left[l, c]
        pt_out[l] = total
        hi, lo = split(total)
        lhl[0:rank, :] = hi
        lhl[rank:, :] = lo
        gram[l, row, :, 0:rank] = dot(total, total, NT, HIGHEST)
        for d in range(1, nr):
            r = lax.rem(row + d, nr)
            send(gram.at[l, row], gram.at[l, row], sg_s.at[l, r], sg_r.at[l, row], row=r).start()

    def sib_copy(l, dz, j):
        return send(rpart.at[l, j], rsib.at[l, dz], ss_s.at[l, dz], ss_r.at[l, dz], row=sib)

    def z_copy(l, dz, slot):
        j = dz * 2 + core
        return send(rpart.at[l, j], rz.at[l, slot], sz_s.at[l, dz], sz_r.at[l, slot], row=j)

    def right(l):
        def join(dz):
            sib_copy(l, dz, dz * 2 + core).wait_recv()
            rpart[l, dz * 2 + core] += rsib[l, dz]

        def step(i, _):
            dz = peer(1 + i)

            def chunk(e, _):
                j = dz * 2 + lax.rem(core + 1 + e, 2)
                mh, ml = split(mbuf[l, :, cols(j)])
                both = dot(lhl[...], mh) + dot(lhl[...], ml)
                rpart[l, j] = both[0:rank] + both[rank:]

                @pl.when(e == 0)
                def _():
                    sib_copy(l, dz, j).start()

                return 0

            lax.fori_loop(0, 2, chunk, 0)

            @pl.when(i > 0)
            def _():
                join(peer(i))
                z_copy(l, peer(i), z).start()

            return 0

        lax.fori_loop(0, nz, step, 0)
        join(z)

    def solve(l):
        for d in range(1, nr):
            r = lax.rem(row + d, nr)
            send(gram.at[l, r], gram.at[l, r], sg_s.at[l, r], sg_r.at[l, r], row=r).wait()
        total = gram[l, 0]
        for r in range(1, nr):
            total = total + gram[l, r]
        linv[l] = inverse_factor(total[:, 0:rank])

    def new_copy(l, r, slot):
        return send(qnew.at[slot, l], qnew.at[slot, l], sn_s.at[l, r], sn_r.at[l, slot], row=r)

    def new_forward(l, slot):
        return send(qnew.at[slot, l], qnew.at[slot, l], sm_s.at[l, slot], sn_r.at[l, slot], row=sib)

    def own(l):
        total = rpart[l, row]
        for d in range(1, nz):
            z_copy(l, peer(d), peer(d)).wait_recv()
            total = total + rz[l, peer(d)]
        qnew[row, l] = dot(linv[l], total, NN, HIGHEST)
        new_copy(l, sib, row).start()
        for d in range(1, nz):
            new_copy(l, peer(d) * 2 + core, row).start()

    def left_out(l):
        hat = dot(linv[l], pt_out[l], NN, HIGHEST)
        pt_out[l] = hat
        hi, lo = split(hat)
        stack = jnp.concatenate([hi, lo, hi], axis=0)
        for t in range(rows // tile):
            turned = dot(eye(tile, rows, t * tile).astype(jnp.bfloat16), stack, NT)
            pcat_out[l, t * tile : (t + 1) * tile, :] = turned.astype(jnp.bfloat16)

    def forward(l):
        for d in range(1, nz):
            slot = peer(d) * 2 + core
            new_copy(l, slot, slot).wait_recv()
            new_forward(l, slot).start()

    for l in range(layers):
        first(l)
    join_left(0)
    right(0)
    solve(0)
    for l in range(1, layers):
        join_left(l)
        own(l - 1)
        right(l)
        solve(l)
        forward(l - 1)
    own(layers - 1)
    for l in range(layers):
        left_out(l)
    forward(layers - 1)
    for l in range(layers):
        for d in range(nz):
            slot = peer(d) * 2 + (1 - core)
            new_copy(l, sib, slot).wait_recv()

    q_copy(sib, row).wait_send()
    for d in range(1, nz):
        q_copy(peer(d) * 2 + core, row).wait_send()
        q_forward(peer(d) * 2 + core).wait_send()
    for d in range(1, nc):
        p_copy(lax.rem(col + d, nc)).wait_send()
    for l in range(layers):
        new_copy(l, sib, row).wait_send()
        for d in range(nz):
            sib_copy(l, peer(d), peer(d) * 2 + core).wait_send()
        for d in range(1, nz):
            z_copy(l, peer(d), z).wait_send()
            new_copy(l, peer(d) * 2 + core, row).wait_send()
            new_forward(l, peer(d) * 2 + core).wait_send()

    def end(k, _):
        for l in range(layers):
            put(l, k).wait()
        return 0

    lax.fori_loop(0, nr, end, 0)


def error_kernel(pcat, q, m, out):
    rows = m.shape[1]
    tile = row_tile(rows)
    hi, lo = split(q[0, 0])
    both = jnp.concatenate([hi, hi, lo], axis=0)

    def part(t, _):
        at = pl.ds(pl.multiple_of(t * tile, tile), tile)
        out[0, at, :] = m[0, at, :] - dot(pcat[0, at, :], both)
        return 0

    lax.fori_loop(0, rows // tile, part, 0)


def shards(nr, nc, grad, memory, p_prev, q_prev):
    layers, rows, columns = grad.shape
    rank, share, width = p_prev.shape[2], p_prev.shape[1], q_prev.shape[1]
    nz = nr // 2
    f32, bf16 = jnp.float32, jnp.bfloat16
    dma = pltpu.SemaphoreType.DMA
    anyspace = pl.BlockSpec(memory_space=pl.ANY)
    vmem = pl.BlockSpec(memory_space=pltpu.VMEM)
    merged, pcat, pt, qnew = pl.pallas_call(
        functools.partial(exchange_kernel, nr, nc, layers),
        out_shape=(
            jax.ShapeDtypeStruct((layers, rows, columns), f32),
            jax.ShapeDtypeStruct((layers, rows, 3 * rank), bf16),
            jax.ShapeDtypeStruct((layers, rank, rows), f32),
            jax.ShapeDtypeStruct((nr, layers, rank, width), f32),
        ),
        in_specs=[anyspace, anyspace, vmem, vmem],
        out_specs=(anyspace, vmem, vmem, vmem),
        scratch_shapes=[
            pltpu.VMEM((layers, rows, columns), f32),
            pltpu.VMEM((rows, columns), bf16),
            pltpu.VMEM((nc, layers, rank, share), f32),
            pltpu.VMEM((nr, layers, rank, width), f32),
            pltpu.VMEM((layers, rows, 3 * rank), bf16),
            pltpu.VMEM((3 * rank, width), bf16),
            pltpu.VMEM((layers, rows, 2 * rank), f32),
            pltpu.VMEM((layers, nc, rank, rows), f32),
            pltpu.VMEM((2 * rank, rows), bf16),
            pltpu.VMEM((layers, nr, rank, 128), f32),
            pltpu.VMEM((layers, nr, rank, width), f32),
            pltpu.VMEM((layers, nz, rank, width), f32),
            pltpu.VMEM((layers, nz, rank, width), f32),
            pltpu.VMEM((layers, rank, rank), f32),
            dma((layers, nr)), dma((layers, nr)), dma((layers, nr)),
            dma((nc,)), dma((nc,)), dma((nr,)), dma((nr,)), dma((nr,)),
            dma((layers, nc)), dma((layers, nc)), dma((layers, nr)), dma((layers, nr)),
            dma((layers, nz)), dma((layers, nz)), dma((layers, nz)), dma((layers, nz)),
            dma((layers, nr)), dma((layers, nr)), dma((layers, nr)),
        ],
        compiler_params=pltpu.CompilerParams(
            collective_id=0, has_side_effects=True, vmem_limit_bytes=VMEM_BYTES
        ),
        name="exchange",
    )(grad, memory, jnp.swapaxes(p_prev, 1, 2), jnp.swapaxes(q_prev, 1, 2))
    error = pl.pallas_call(
        error_kernel,
        grid=(layers, nr),
        out_shape=jax.ShapeDtypeStruct((layers, rows, columns), f32),
        in_specs=[
            pl.BlockSpec((1, rows, 3 * rank), lambda l, j: (l, 0, 0)),
            pl.BlockSpec((1, 1, rank, width), lambda l, j: (j, l, 0, 0)),
            pl.BlockSpec((1, rows, width), lambda l, j: (l, 0, j)),
        ],
        out_specs=pl.BlockSpec((1, rows, width), lambda l, j: (l, 0, j)),
        compiler_params=pltpu.CompilerParams(dimension_semantics=("arbitrary", "arbitrary")),
        name="error",
    )(pcat, qnew, merged)
    p_mine = lax.dynamic_slice_in_dim(pt, lax.axis_index("col") * share, share, 2)
    q_mine = lax.dynamic_index_in_dim(qnew, lax.axis_index("row"), 0, keepdims=False)
    return jnp.swapaxes(p_mine, 1, 2), jnp.swapaxes(q_mine, 1, 2), error


def plain_shards(grad, memory, p_prev, q_prev):
    left_rows = lax.all_gather(p_prev, "col", axis=1, tiled=True)
    right_rows = lax.all_gather(q_prev, "row", axis=1, tiled=True)
    approx = jnp.einsum("lrk,lck->lrc", left_rows, right_rows, precision=HIGHEST)
    merged = grad.astype(jnp.float32) + memory - approx
    partial_value = jnp.einsum("lrc,lck->lrk", merged, right_rows, precision=HIGHEST)
    left = lax.psum(partial_value, "col")
    gram = lax.psum(jnp.einsum("lrk,lrj->lkj", left, left, precision=HIGHEST), "row")
    factor = jnp.linalg.cholesky(gram)
    p_hat = lax.linalg.triangular_solve(factor, left, left_side=False, lower=True, transpose_a=True)
    right_part = jnp.einsum("lrc,lrk->lck", merged, p_hat, precision=HIGHEST)
    share_rows = right_part.shape[1] // lax.axis_size("row")
    right_full = lax.psum(right_part, "row")
    q_new = lax.dynamic_slice_in_dim(right_full, lax.axis_index("row") * share_rows, share_rows, 1)
    error = merged - jnp.einsum("lrk,lck->lrc", p_hat, right_full, precision=HIGHEST)
    left_share = p_hat.shape[1] // lax.axis_size("col")
    p_new = lax.dynamic_slice_in_dim(p_hat, lax.axis_index("col") * left_share, left_share, 1)
    return (p_new, q_new, error)


def solution(mesh):
    nr, nc = mesh.shape["row"], mesh.shape["col"]

    def local(grad, memory, p_prev, q_prev):
        if q_prev.shape[1] % 128 or p_prev.shape[1] % 16 or nr % 2:
            return plain_shards(grad, memory, p_prev, q_prev)
        return shards(nr, nc, grad, memory, p_prev, q_prev)

    placed = (
        P(None, "row", "col"),
        P(None, "row", "col"),
        P(None, ("row", "col"), None),
        P(None, ("col", "row"), None),
    )
    return jax.shard_map(
        local,
        mesh=mesh,
        in_specs=placed,
        out_specs=(
            P(None, ("row", "col"), None),
            P(None, ("col", "row"), None),
            P(None, "row", "col"),
        ),
        check_vma=False,
    )
```
